32 devices in a mesh: src: 4 (over z), space: 8 (over y, x, core).
Axes of the slice: x: 2, y: 2, z: 4, core: 2. Of those that a mesh axis runs over, the one named last changes fastest.
Arguments:
- background: float32 [2, 4, 3, 16, 32, 128], P(None, 'src', None, 'space'), may hold values from -6 to 6
- warm_start: float32 [2, 4, 3, 16, 32, 128], P(None, 'src', None, 'space'), may hold values from -0.15625 to 0.15625
- conductivity: float32 [16, 32, 128], P('space'), may hold values from 0.3 to 3
- frequencies: float32 [8], replicated, may hold values from 0.1 to 1
- pair_freq: int32 [4], P('src'), may hold values from 0 to 7
- weighted_residual: float32 [2, 4, 1024], P(None, 'src', 'space'), may hold values from -6 to 6
- datum_layer_index: int32 [1024, 1], replicated, may hold values from 0 to 7; in each aligned block of 128 rows (0 to 127, 128 to 255, ...) at most 32 rows name the same one
- receiver_flat_cell: int32 [1024], replicated, may hold values from 0 to 8191
- receiver_component: int32 [1024], replicated, may hold values from 0 to 2
Outputs:
- adjoint: float32 [2, 4, 3, 16, 32, 128], P(None, 'src', None, 'space')
- gradient: float32 [16, 32, 128], P('space', 'src')
The draws below stay inside these ranges and needn't reach their ends.
Inputs may be any that keep to these rules, and one draw needn't show every extreme that they name: `datum_layer_index`: among the 128 measurements of each aligned block (the measurements of one device), no slab is named by more than 32 of them, a bound that some block reaches.
All inputs are finite; a program needn't handle non-finite values.
Results may differ from the reference program's by a relative error of at most 0.0001.
Values sent between devices are 32-bit elements; how exact they have to be, the bound alone decides.
A program may use at most 64 MiB of HBM per device.

```python
import math
import jax
import jax.numpy as jnp
import numpy as np
from jax import lax

SLAB_PLANES = 2
CELLS_SECOND = 32
CELLS_THIRD = 128
DATA_PER_SITE = 128
NFREQ = 8
ITERS = 4
SOURCE_FREQ_PAIRS = 4
NX = 16
DATUM_TOTAL = 1024
LAYER_DATUM_CAP = 32
N_SPACE = 8


def plant(result, rng, low, largest):
    longest = result.shape.index(max(result.shape))
    spots = []
    for shift in (0, 1):
        where = [jax.random.randint(jax.random.fold_in(rng, axis), (), 0, length) for axis, length in enumerate(result.shape)]
        where[longest] = (where[longest] + shift) % result.shape[longest]
        spots.append(tuple(where))
    return result.at[spots[0]].set(low).at[spots[1]].set(largest)


def shard_levels(rng, dims, pieces, least, largest):
    level = 1.0
    for position, parts in pieces:
        heights = jax.random.uniform(jax.random.fold_in(jax.random.fold_in(rng, 6), position), (parts,), jnp.float32, least / len(pieces), largest / len(pieces))
        level = level * jnp.repeat(jnp.exp(heights), dims[position] // parts).reshape((-1,) + (1,) * (len(dims) - 1 - position))
    return level


def shared_out(key, own, number, rows, count, top, most, slope):
    ranking = jax.random.permutation(key, count)
    packed, usual = portions_of(count, rows * top, most, slope, True), portions_of(count, rows * top, most, slope, False)
    places = jnp.arange(count)

    def named(sizes, rotation):
        used = int((sizes > 0).sum())
        fixed = max(1, used // 4)
        passed = fixed + (places - fixed + rotation * (used - fixed)) % max(1, count - fixed)
        return jnp.zeros((count,), jnp.int32).at[ranking[jnp.where(places < fixed, places, passed)]].set(jnp.asarray(sizes, jnp.int32))

    sizes = jnp.where(number % 4 == 0, named(packed, number // 4), named(usual, number - number // 4 - 1))
    mixed = jax.random.permutation(jax.random.fold_in(own, 3), count)
    donor, sink = mixed[0:count // 2 * 2:2], mixed[1:count // 2 * 2:2]
    slack = jnp.minimum(sizes[donor] - 1, most - sizes[sink]) // 2
    slack = jnp.where((donor == ranking[0]) | (sink == ranking[0]) | (sizes[sink] == 0), 0, jnp.maximum(slack, 0))
    passed = jax.random.randint(jax.random.fold_in(own, 4), (count // 2,), 0, 1 << 20) % (slack + 1)
    sizes = sizes.at[donor].add(-passed).at[sink].add(passed)
    members = jnp.searchsorted(jnp.cumsum(sizes), jnp.arange(rows * top), side="right").astype(jnp.int32)
    grid = members.reshape(top, rows).T
    grid = grid[jax.random.permutation(jax.random.fold_in(own, 1), rows)]
    rotation = jax.random.randint(jax.random.fold_in(own, 2), (rows, 1), 0, top)
    return jnp.take_along_axis(grid, (jnp.arange(top)[None, :] + rotation) % top, axis=1)


def portions_of(amount, total, bound, skew, full):
    weights = [(1 << 20) // math.isqrt(rank ** skew) + 1 for rank in range(1, amount + 1)]
    largest = bound if full else min(bound, max(-(-total // amount), total * weights[0] // sum(weights)))
    least = 1 if total - largest >= amount - 1 else 0
    counts, surplus = [largest] + [least] * (amount - 1), total - largest - least * (amount - 1)
    while surplus > 0:
        free = [i for i in range(1, amount) if counts[i] < largest] or [i for i in range(1, amount) if counts[i] < bound]
        mass, left = sum([weights[i] for i in free]), surplus
        for i in free:
            more = min(bound - counts[i], max(1, left * weights[i] // mass), surplus)
            counts[i] = counts[i] + more
            surplus = surplus - more
    return np.array(counts)


def normal_values(own_key, dims, spread, limit, cuts=(), dtype=jnp.bfloat16):
    drawn = spread * jax.random.normal(own_key, dims, jnp.float32)
    if cuts:
        drawn = drawn * shard_levels(own_key, dims, cuts, -0.22, 0.18)
    return jnp.clip(drawn, -limit, limit).astype(dtype)


def setup_inputs(seed: int = 0) -> dict:
    splits = jax.random.split(jax.random.key(seed), 10)
    background = normal_values(splits[0], (2, SOURCE_FREQ_PAIRS, 3, NX, CELLS_SECOND, CELLS_THIRD), 1.0, 6.0, ((1, 4), (3, 8)), jnp.float32)
    warm_start = normal_values(splits[1], (2, SOURCE_FREQ_PAIRS, 3, NX, CELLS_SECOND, CELLS_THIRD), 0.01, 0.15625, ((1, 4), (3, 8)), jnp.float32)
    conductivity = jnp.clip(jnp.exp(math.log(3.0) - 2.3025851 * jax.random.uniform(splits[2], (NX, CELLS_SECOND, CELLS_THIRD), jnp.float32) ** shard_levels(splits[2], (NX, CELLS_SECOND, CELLS_THIRD), ((0, 8),), -0.2, 0.2)), 0.3, 3.0)
    frequencies = jnp.clip(jnp.exp(jax.random.uniform(splits[3], (NFREQ,), jnp.float32, math.log(0.1), math.log(1.0))), 0.1, 1.0)
    pair_freq = plant(jax.random.randint(splits[4], (SOURCE_FREQ_PAIRS,), 0, NFREQ), jax.random.fold_in(splits[4], 1), 0, NFREQ - 1).astype(jnp.int32)
    weighted_residual = normal_values(splits[5], (2, SOURCE_FREQ_PAIRS, DATUM_TOTAL), 1.0, 6.0, ((1, 4), (2, 8)), jnp.float32)
    datum_layer_index_keys = jax.random.split(jax.random.fold_in(splits[6], 1), DATUM_TOTAL // DATA_PER_SITE)
    datum_layer_index_turns = jax.random.permutation(jax.random.fold_in(splits[6], 3), DATUM_TOTAL // DATA_PER_SITE)
    datum_layer_index = jax.vmap(lambda own, number: shared_out(jax.random.fold_in(splits[6], 2), own, number, DATA_PER_SITE, N_SPACE, 1, LAYER_DATUM_CAP, 2))(datum_layer_index_keys, datum_layer_index_turns).reshape((DATUM_TOTAL, 1))
    receiver_flat_cell = plant(jax.random.randint(splits[7], (DATUM_TOTAL,), 0, SLAB_PLANES * CELLS_SECOND * CELLS_THIRD), jax.random.fold_in(splits[7], 1), 0, (SLAB_PLANES * CELLS_SECOND * CELLS_THIRD) - 1).astype(jnp.int32)
    receiver_component = plant(jax.random.randint(splits[8], (DATUM_TOTAL,), 0, 3), jax.random.fold_in(splits[8], 1), 0, 2).astype(jnp.int32)
    return dict(background=background, warm_start=warm_start, conductivity=conductivity, frequencies=frequencies, pair_freq=pair_freq, weighted_residual=weighted_residual, datum_layer_index=datum_layer_index, receiver_flat_cell=receiver_flat_cell, receiver_component=receiver_component)


def diff_forward(field, spatial):
    base = field[..., :-1, :-1, :-1]
    if spatial == 0:
        return field[..., 1:, :-1, :-1] - base
    if spatial == 1:
        return field[..., :-1, 1:, :-1] - base
    return field[..., :-1, :-1, 1:] - base


def diff_backward(field, spatial):
    base = field[..., 1:, 1:, 1:]
    if spatial == 0:
        return base - field[..., :-1, 1:, 1:]
    if spatial == 1:
        return base - field[..., 1:, :-1, 1:]
    return base - field[..., 1:, 1:, :-1]


def curl_forward(padded):
    comp_x = padded[..., 0, :, :, :]
    comp_y = padded[..., 1, :, :, :]
    comp_z = padded[..., 2, :, :, :]
    mag_x = diff_forward(comp_z, 1) - diff_forward(comp_y, 2)
    mag_y = diff_forward(comp_x, 2) - diff_forward(comp_z, 0)
    mag_z = diff_forward(comp_y, 0) - diff_forward(comp_x, 1)
    return jnp.stack([mag_x, mag_y, mag_z], axis=-4)


def curl_backward(magnetic):
    mag_x = magnetic[..., 0, :, :, :]
    mag_y = magnetic[..., 1, :, :, :]
    mag_z = magnetic[..., 2, :, :, :]
    out_x = diff_backward(mag_z, 1) - diff_backward(mag_y, 2)
    out_y = diff_backward(mag_x, 2) - diff_backward(mag_z, 0)
    out_z = diff_backward(mag_y, 0) - diff_backward(mag_x, 1)
    return jnp.stack([out_x, out_y, out_z], axis=-4)


def operate(field, damping):
    padded = jnp.pad(field, ((0, 0), (0, 0), (1, 1), (1, 1), (1, 1)))
    curled = curl_backward(curl_forward(padded))
    return jnp.stack([curled[0] - damping * field[1], curled[1] + damping * field[0]])


def inner(first_vec, second_vec):
    real_part = jnp.sum(first_vec[0] * second_vec[0] + first_vec[1] * second_vec[1])
    quadrature_share = jnp.sum(first_vec[0] * second_vec[1] - first_vec[1] * second_vec[0])
    return real_part, quadrature_share


def scaled(coef_re, coef_im, field):
    return jnp.stack([coef_re * field[0] - coef_im * field[1], coef_re * field[1] + coef_im * field[0]])


def solve_pair(start, source, damping):
    adjoint = start
    residual = source - operate(adjoint, damping)
    direction = residual
    mapped = operate(direction, damping)
    for sweep in range(ITERS):
        mixed_product_real, cross_im = inner(mapped, residual)
        projected_magnitude = jnp.sum(mapped * mapped)
        alpha_re = mixed_product_real / projected_magnitude
        alpha_im = cross_im / projected_magnitude
        adjoint = adjoint + scaled(alpha_re, alpha_im, direction)
        residual = residual - scaled(alpha_re, alpha_im, mapped)
        if sweep + 1 < ITERS:
            fresh = operate(residual, damping)
            turn_re, turn_im = inner(mapped, fresh)
            beta_re = -turn_re / projected_magnitude
            beta_im = -turn_im / projected_magnitude
            direction = residual + scaled(beta_re, beta_im, direction)
            mapped = fresh + scaled(beta_re, beta_im, mapped)
    return adjoint


def reference(background, warm_start, conductivity, frequencies, pair_freq, weighted_residual, datum_layer_index, receiver_flat_cell, receiver_component):
    total_cells = NX * CELLS_SECOND * CELLS_THIRD
    slab_cells = SLAB_PLANES * CELLS_SECOND * CELLS_THIRD
    target = (receiver_component * total_cells + datum_layer_index[:, 0] * slab_cells + receiver_flat_cell).astype(jnp.int32)
    flat_src = jnp.zeros((2, SOURCE_FREQ_PAIRS, 3 * total_cells), jnp.float32).at[:, :, target].add(weighted_residual)
    source = flat_src.reshape(2, SOURCE_FREQ_PAIRS, 3, NX, CELLS_SECOND, CELLS_THIRD)
    wave_k = frequencies[pair_freq.astype(jnp.int32)]
    items = (jnp.moveaxis(warm_start, 1, 0), jnp.moveaxis(source, 1, 0), jnp.moveaxis(background, 1, 0), wave_k)

    def one_pair(total, item):
        start, pair_src, pair_bg, pair_k = item
        adjoint = solve_pair(start, pair_src, pair_k * conductivity)
        total = total + pair_k * jnp.sum(adjoint[0] * pair_bg[1] + adjoint[1] * pair_bg[0], axis=0)
        return total, adjoint

    gradient, adjoints = lax.scan(one_pair, jnp.zeros((NX, CELLS_SECOND, CELLS_THIRD), jnp.float32), items)
    return jnp.moveaxis(adjoints, 0, 1), gradient
```

```python
import functools

import jax
import jax.numpy as jnp
from jax import lax
from jax.experimental import pallas as pl
from jax.experimental.pallas import tpu as pltpu
from jax.sharding import PartitionSpec as P

ITERS = 4
SHIFT = 6.0
MESH = pl.DeviceIdType.MESH


def up(field, axis):
    length = field.shape[axis]
    cell = lax.broadcasted_iota(jnp.int32, field.shape, axis)
    return jnp.where(cell == length - 1, 0.0, pltpu.roll(field, length - 1, axis))


def down(field, axis, first):
    cell = lax.broadcasted_iota(jnp.int32, field.shape, axis)
    return jnp.where(cell == 0, first, pltpu.roll(field, 1, axis))


def edge_sums(comp_x, comp_y, comp_z):
    return comp_y + (up(comp_x, 1) - comp_x), comp_z + (up(comp_x, 2) - comp_x)


def curl_curl(comp_x, comp_y, comp_z):
    zero = jnp.zeros_like(comp_x[:1])
    sum_y, sum_z = edge_sums(comp_x, comp_y, comp_z)
    mag_z = jnp.concatenate([comp_y[1:], zero]) - sum_y
    mag_y = sum_z - jnp.concatenate([comp_z[1:], zero])
    mag_x = (up(comp_z, 1) - comp_z) - (up(comp_y, 2) - comp_y)
    before_z = jnp.concatenate([comp_y[:1], mag_z[:-1]])
    before_y = jnp.concatenate([-comp_z[:1], mag_y[:-1]])
    out_x = (mag_z - down(mag_z, 1, -comp_x)) - (mag_y - down(mag_y, 2, comp_x))
    out_y = (mag_x - down(mag_x, 2, -comp_y)) - (mag_z - before_z)
    out_z = (mag_y - before_y) - (mag_x - down(mag_x, 1, comp_z))
    return out_x, out_y, out_z


def c_mul(a, b):
    return a[0] * b[0] - a[1] * b[1], a[0] * b[1] + a[1] * b[0]


def c_add(a, b):
    return a[0] + b[0], a[1] + b[1]


def c_sum(terms):
    total = terms[0]
    for term in terms[1:]:
        total = c_add(total, term)
    return total


def gram_slots():
    slots = {}
    for k in range(ITERS + 1):
        for j in range(k + 1):
            slots[j, k, 0] = len(slots)
            if j < k:
                slots[j, k, 1] = len(slots)
    return slots


def combination(gram):
    zero = jnp.zeros_like(gram(0, 0)[0])
    one = zero + 1.0

    def dot(left, right):
        return c_sum([c_mul(a, b) for a, b in zip(left, right)])

    def operate(vec):
        shifted = [(SHIFT * a, SHIFT * b) for a, b in vec] + [(zero, zero)]
        return [shifted[0]] + [c_add(s, v) for s, v in zip(shifted[1:], vec)]

    def axpy(coef, vec, base):
        base = list(base) + [(zero, zero)] * (len(vec) - len(base))
        moved = [c_add(b, c_mul(coef, v)) for v, b in zip(vec, base)]
        return moved + base[len(vec):]

    residual = [(one, zero)]
    direction = residual
    mapped = operate(direction)
    update = [(zero, zero)]
    for sweep in range(ITERS):
        weights = [
            c_sum([c_mul((m[0], -m[1]), gram(j, k)) for j, m in enumerate(mapped)])
            for k in range(min(len(mapped) + 1, ITERS + 1))
        ]
        norm = dot(weights[: len(mapped)], mapped)[0]
        mixed = dot(weights, residual)
        alpha = (mixed[0] / norm, mixed[1] / norm)
        update = axpy(alpha, direction, update)
        if sweep + 1 < ITERS:
            residual = axpy((-alpha[0], -alpha[1]), mapped, residual)
            fresh = operate(residual)
            turn = dot(weights, fresh)
            beta = (-turn[0] / norm, -turn[1] / norm)
            direction = axpy(beta, direction, residual)
            mapped = axpy(beta, mapped, fresh)
    return update


def kernel(
    n_space,
    n_src,
    background,
    warm,
    conductivity,
    frequencies,
    pair_freq,
    measured,
    layer,
    cell,
    component,
    adjoint,
    gradient,
    basis,
    sums,
    above,
    below,
    source,
    measured_all,
    gram_rows,
    gram_all,
    shares,
    shares_in,
    halo_send,
    halo_recv,
    measured_send,
    measured_recv,
    gram_send,
    gram_recv,
    share_send,
    share_recv,
):
    me = lax.axis_index("space")
    pair = lax.axis_index("src")
    planes, rows_y, rows_z = conductivity.shape
    last = planes - 1

    barrier = pltpu.get_barrier_semaphore()
    for off in range(1, n_space):
        pl.semaphore_signal(
            barrier, 1, device_id={"space": lax.rem(me + off, n_space)}, device_id_type=MESH
        )
    for off in range(1, n_src):
        pl.semaphore_signal(
            barrier, 1, device_id={"src": lax.rem(pair + off, n_src)}, device_id_type=MESH
        )

    wave_k = frequencies[pair_freq[0]]

    def store_sums(field):
        for part in range(2):
            sum_y, sum_z = edge_sums(
                field(part, 0)[last:], field(part, 1)[last:], field(part, 2)[last:]
            )
            sums[part, 0] = sum_y[0]
            sums[part, 1] = sum_z[0]

    def warm_field(part, comp):
        return warm[part, 0, comp]

    def basis_field(index):
        return lambda part, comp: basis[index, part, comp]

    @pl.when(me == 0)
    def _():
        below[...] = jnp.zeros_like(below)

    @pl.when(me == n_space - 1)
    def _():
        above[...] = jnp.zeros_like(above)

    for part in range(2):
        sum_y, sum_z = edge_sums(*[warm[part, 0, c][last:] for c in range(3)])
        sums[0, part, 0] = sum_y[0]
        sums[0, part, 1] = sum_z[0]

    pl.semaphore_wait(barrier, n_space - 1 + n_src - 1)

    def halo_copies(step):
        first = warm.at[:, 0, pl.ds(1, 2), 0] if step == 0 else basis.at[step - 1, :, pl.ds(1, 2), 0]
        upward = pltpu.make_async_remote_copy(
            src_ref=sums.at[step],
            dst_ref=below.at[step],
            send_sem=halo_send.at[step, 0],
            recv_sem=halo_recv.at[step, 0],
            device_id={"space": lax.rem(me + 1, n_space)},
            device_id_type=MESH,
        )
        downward = pltpu.make_async_remote_copy(
            src_ref=first,
            dst_ref=above.at[step],
            send_sem=halo_send.at[step, 1],
            recv_sem=halo_recv.at[step, 1],
            device_id={"space": lax.rem(me + n_space - 1, n_space)},
            device_id_type=MESH,
        )
        return upward, downward

    def start_halo(step):
        upward, downward = halo_copies(step)

        @pl.when(me < n_space - 1)
        def _():
            upward.start()

        @pl.when(me > 0)
        def _():
            downward.start()

    def wait_halo(step):
        upward, downward = halo_copies(step)

        @pl.when(me > 0)
        def _():
            upward.wait_recv()

        @pl.when(me < n_space - 1)
        def _():
            downward.wait_recv()

    def end_halo(step):
        upward, downward = halo_copies(step)

        @pl.when(me < n_space - 1)
        def _():
            upward.wait_send()

        @pl.when(me > 0)
        def _():
            downward.wait_send()

    def measured_copy(off):
        return pltpu.make_async_remote_copy(
            src_ref=measured,
            dst_ref=measured_all.at[off],
            send_sem=measured_send.at[off],
            recv_sem=measured_recv.at[off],
            device_id={"space": lax.rem(me + off, n_space)},
            device_id_type=MESH,
        )

    def gram_copy(off):
        return pltpu.make_async_remote_copy(
            src_ref=gram_all.at[me],
            dst_ref=gram_all.at[me],
            send_sem=gram_send.at[off],
            recv_sem=gram_recv.at[off],
            device_id={"space": lax.rem(me + off, n_space)},
            device_id_type=MESH,
        )

    def gram_arrival(off):
        return pltpu.make_async_remote_copy(
            src_ref=gram_all.at[me],
            dst_ref=gram_all.at[lax.rem(me + n_space - off, n_space)],
            send_sem=gram_send.at[off],
            recv_sem=gram_recv.at[off],
            device_id={"space": lax.rem(me + off, n_space)},
            device_id_type=MESH,
        )

    def share_copy(off):
        peer = lax.rem(pair + off, n_src)
        return pltpu.make_async_remote_copy(
            src_ref=shares.at[peer],
            dst_ref=shares_in.at[off],
            send_sem=share_send.at[off],
            recv_sem=share_recv.at[off],
            device_id={"src": peer},
            device_id_type=MESH,
        )

    for off in range(1, n_space):
        measured_copy(off).start()
    start_halo(0)

    damping = wave_k * conductivity[...]

    for part in range(2):
        curled = curl_curl(*[warm[part, 0, c] for c in range(3)])
        for c in range(3):
            turned = damping * warm[1 - part, 0, c]
            basis[0, part, c] = -(curled[c] - turned if part == 0 else curled[c] + turned)

    for off in range(1, n_space):
        measured_copy(off).wait_recv()
    shift_z = rows_z.bit_length() - 1
    row_count = 3 * planes * rows_y
    sites = measured.shape[2]
    row_id = lax.broadcasted_iota(jnp.int32, (row_count, sites), 0)
    lane_id = lax.broadcasted_iota(jnp.int32, (rows_z, sites), 0)
    row_hot = []
    pieces = [[] for _ in range(6)]
    for off in range(n_space):
        sender = lax.rem(me + n_space - off, n_space)
        owner = layer[pl.ds(sender, 1), :]
        where_cell = cell[pl.ds(sender, 1), :]
        row = component[pl.ds(sender, 1), :] * (planes * rows_y) + lax.shift_right_logical(
            where_cell, shift_z
        )
        row = jnp.where(owner == me, row, -1)
        row_hot.append(jnp.where(row_id == row, 1.0, 0.0).astype(jnp.bfloat16))
        lane_hit = lane_id == jnp.bitwise_and(where_cell, rows_z - 1)
        for part in range(2):
            value = measured[part] if off == 0 else measured_all[off, part]
            rest = value
            for piece in range(3):
                rounded = rest.astype(jnp.bfloat16).astype(jnp.float32)
                rest = rest - rounded
                pieces[part * 3 + piece].append(
                    jnp.where(lane_hit, rounded, 0.0).astype(jnp.bfloat16)
                )
    hot = jnp.concatenate(row_hot, axis=1)
    for part in range(2):
        total = None
        for piece in range(3):
            term = lax.dot_general(
                hot,
                jnp.concatenate(pieces[part * 3 + piece], axis=1),
                (((1,), (1,)), ((), ())),
                preferred_element_type=jnp.float32,
            )
            total = term if total is None else total + term
        source[part] = total.reshape(3, planes, rows_y, rows_z)
    for part in range(2):
        for c in range(3):
            basis[0, part, c] = basis[0, part, c] + source[part, c]

    slots = gram_slots()
    cells = 3 * planes * rows_y

    def gram_column(k):
        for j in range(k + 1):
            left = [basis[j, part].reshape(cells, rows_z) for part in range(2)]
            right = [basis[k, part].reshape(cells, rows_z) for part in range(2)]
            spot = slots[j, k, 0]
            gram_rows[spot : spot + 1, :] = jnp.sum(
                left[0] * right[0] + left[1] * right[1], axis=0, keepdims=True
            )
            if j < k:
                spot = slots[j, k, 1]
                gram_rows[spot : spot + 1, :] = jnp.sum(
                    left[0] * right[1] - left[1] * right[0], axis=0, keepdims=True
                )

    def correct(step, sign):
        for part in range(2):
            over_y = sign * above[step, part, 0]
            over_z = sign * above[step, part, 1]
            slope = (over_y - down(over_y, 0, 0.0)) + (over_z - down(over_z, 1, 0.0))
            basis[step, part, 0, last] = basis[step, part, 0, last] + slope
            basis[step, part, 1, last] = basis[step, part, 1, last] - over_y
            basis[step, part, 2, last] = basis[step, part, 2, last] - over_z
            basis[step, part, 1, 0] = basis[step, part, 1, 0] - sign * below[step, part, 0]
            basis[step, part, 2, 0] = basis[step, part, 2, 0] - sign * below[step, part, 1]

    for k in range(ITERS + 1):
        wait_halo(k)
        correct(k, -1.0 if k == 0 else 1.0)
        if k < ITERS:
            for part in range(2):
                sum_y, sum_z = edge_sums(*[basis[k, part, c][last:] for c in range(3)])
                sums[k + 1, part, 0] = sum_y[0]
                sums[k + 1, part, 1] = sum_z[0]
            start_halo(k + 1)
            for part in range(2):
                curled = curl_curl(*[basis[k, part, c] for c in range(3)])
                for c in range(3):
                    turned = damping * basis[k, 1 - part, c]
                    moved = curled[c] - SHIFT * basis[k, part, c]
                    basis[k + 1, part, c] = moved - turned if part == 0 else moved + turned
        gram_column(k)

    count = len(slots)
    held = gram_rows.shape[0]
    lanes = lax.broadcasted_iota(jnp.int32, (held, rows_z), 1)
    rows = lax.broadcasted_iota(jnp.int32, (held, rows_z), 0)
    row_sums = jnp.sum(jnp.where(rows < count, gram_rows[...], 0.0), axis=1, keepdims=True)
    gram_all[me] = jnp.sum(jnp.where(lanes == rows, row_sums, 0.0), axis=0, keepdims=True)
    for off in range(1, n_space):
        gram_copy(off).start()
    for off in range(1, n_space):
        gram_arrival(off).wait_recv()
    total = gram_all[0]
    for index in range(1, n_space):
        total = total + gram_all[index]
    splat = {
        key: jnp.broadcast_to(total[:, spot : spot + 1], (8, rows_z)) for key, spot in slots.items()
    }

    def gram(j, k):
        real = splat[min(j, k), max(j, k), 0]
        if j == k:
            return real, jnp.zeros_like(real)
        imag = splat[min(j, k), max(j, k), 1]
        return real, imag if j < k else -imag

    update = combination(gram)

    local = None
    tiles = (planes * rows_y // 8, 8, rows_z)
    for c in range(3):
        real = warm[0, 0, c].reshape(tiles)
        imag = warm[1, 0, c].reshape(tiles)
        for k in range(ITERS):
            field_re = basis[k, 0, c].reshape(tiles)
            field_im = basis[k, 1, c].reshape(tiles)
            coef_re, coef_im = update[k][0][None], update[k][1][None]
            real = real + (coef_re * field_re - coef_im * field_im)
            imag = imag + (coef_re * field_im + coef_im * field_re)
        adjoint[0, 0, c] = real.reshape(planes, rows_y, rows_z)
        adjoint[1, 0, c] = imag.reshape(planes, rows_y, rows_z)
        term = real * background[1, 0, c].reshape(tiles) + imag * background[0, 0, c].reshape(tiles)
        local = term if local is None else local + term
    local = (wave_k * local).reshape(planes, rows_y, rows_z)
    share = rows_y // n_src
    for index in range(n_src):
        shares[index] = local[:, index * share : (index + 1) * share]
    for off in range(1, n_src):
        share_copy(off).start()
    for off in range(1, n_src):
        share_copy(off).wait_recv()
    result = shares[pair]
    for off in range(1, n_src):
        result = result + shares_in[off]
    gradient[...] = result

    for off in range(1, n_space):
        measured_copy(off).wait_send()
    for k in range(ITERS + 1):
        end_halo(k)
    for off in range(1, n_space):
        gram_copy(off).wait_send()
    for off in range(1, n_src):
        share_copy(off).wait_send()


def shards(
    n_space,
    n_src,
    background,
    warm_start,
    conductivity,
    frequencies,
    pair_freq,
    weighted_residual,
    datum_layer_index,
    receiver_flat_cell,
    receiver_component,
):
    planes, rows_y, rows_z = conductivity.shape
    sites = weighted_residual.shape[2]
    held = -(-len(gram_slots()) // 8) * 8
    vmem = pl.BlockSpec(memory_space=pltpu.VMEM)
    smem = pl.BlockSpec(memory_space=pltpu.SMEM)
    f32 = jnp.float32
    dma = pltpu.SemaphoreType.DMA
    return pl.pallas_call(
        functools.partial(kernel, n_space, n_src),
        out_shape=(
            jax.ShapeDtypeStruct(warm_start.shape, f32),
            jax.ShapeDtypeStruct((planes, rows_y // n_src, rows_z), f32),
        ),
        in_specs=[vmem, vmem, vmem, smem, smem, vmem, vmem, vmem, vmem],
        out_specs=(vmem, vmem),
        scratch_shapes=[
            pltpu.VMEM((ITERS + 1, 2, 3, planes, rows_y, rows_z), f32),
            pltpu.VMEM((ITERS + 1, 2, 2, rows_y, rows_z), f32),
            pltpu.VMEM((ITERS + 1, 2, 2, rows_y, rows_z), f32),
            pltpu.VMEM((ITERS + 1, 2, 2, rows_y, rows_z), f32),
            pltpu.VMEM((2, 3, planes, rows_y, rows_z), f32),
            pltpu.VMEM((n_space, 2, 1, sites), f32),
            pltpu.VMEM((held, rows_z), f32),
            pltpu.VMEM((n_space, 1, rows_z), f32),
            pltpu.VMEM((n_src, planes, rows_y // n_src, rows_z), f32),
            pltpu.VMEM((n_src, planes, rows_y // n_src, rows_z), f32),
            dma((ITERS + 1, 2)),
            dma((ITERS + 1, 2)),
            dma((n_space,)),
            dma((n_space,)),
            dma((n_space,)),
            dma((n_space,)),
            dma((n_src,)),
            dma((n_src,)),
        ],
        compiler_params=pltpu.CompilerParams(collective_id=0, has_side_effects=True),
    )(
        background,
        warm_start,
        conductivity,
        frequencies,
        pair_freq,
        weighted_residual,
        datum_layer_index.reshape(n_space, sites),
        receiver_flat_cell.reshape(n_space, sites),
        receiver_component.reshape(n_space, sites),
    )


def solution(mesh):
    placed = (
        P(None, "src", None, "space", None, None),
        P(None, "src", None, "space", None, None),
        P("space", None, None),
        P(),
        P("src"),
        P(None, "src", "space"),
        P(),
        P(),
        P(),
    )
    return jax.shard_map(
        functools.partial(shards, mesh.shape["space"], mesh.shape["src"]),
        mesh=mesh,
        in_specs=placed,
        out_specs=(P(None, "src", None, "space", None, None), P("space", "src", None)),
        check_vma=False,
    )
```

```python
import functools

import jax
import jax.numpy as jnp
from jax import lax
from jax.experimental import pallas as pl
from jax.experimental.pallas import tpu as pltpu
from jax.sharding import PartitionSpec as P

ITERS = 4
SHIFT = 6.0
MESH = pl.DeviceIdType.MESH


def up(field, axis):
    length = field.shape[axis]
    cell = lax.broadcasted_iota(jnp.int32, field.shape, axis)
    return jnp.where(cell == length - 1, 0.0, pltpu.roll(field, length - 1, axis))


def down(field, axis, first):
    cell = lax.broadcasted_iota(jnp.int32, field.shape, axis)
    return jnp.where(cell == 0, first, pltpu.roll(field, 1, axis))


def edge_sums(comp_x, comp_y, comp_z):
    return comp_y + (up(comp_x, 1) - comp_x), comp_z + (up(comp_x, 2) - comp_x)


def curl_curl(comp_x, comp_y, comp_z):
    zero = jnp.zeros_like(comp_x[:1])
    sum_y, sum_z = edge_sums(comp_x, comp_y, comp_z)
    mag_z = jnp.concatenate([comp_y[1:], zero]) - sum_y
    mag_y = sum_z - jnp.concatenate([comp_z[1:], zero])
    mag_x = (up(comp_z, 1) - comp_z) - (up(comp_y, 2) - comp_y)
    before_z = jnp.concatenate([comp_y[:1], mag_z[:-1]])
    before_y = jnp.concatenate([-comp_z[:1], mag_y[:-1]])
    out_x = (mag_z - down(mag_z, 1, -comp_x)) - (mag_y - down(mag_y, 2, comp_x))
    out_y = (mag_x - down(mag_x, 2, -comp_y)) - (mag_z - before_z)
    out_z = (mag_y - before_y) - (mag_x - down(mag_x, 1, comp_z))
    return out_x, out_y, out_z


def c_mul(a, b):
    return a[0] * b[0] - a[1] * b[1], a[0] * b[1] + a[1] * b[0]


def c_add(a, b):
    return a[0] + b[0], a[1] + b[1]


def c_sum(terms):
    total = terms[0]
    for term in terms[1:]:
        total = c_add(total, term)
    return total


def gram_slots():
    slots = {}
    for k in range(ITERS + 1):
        for j in range(k + 1):
            slots[j, k, 0] = len(slots)
            if j < k:
                slots[j, k, 1] = len(slots)
    return slots


def combination(gram):
    zero = jnp.zeros_like(gram(0, 0)[0])
    one = zero + 1.0

    def dot(left, right):
        return c_sum([c_mul(a, b) for a, b in zip(left, right)])

    def operate(vec):
        shifted = [(SHIFT * a, SHIFT * b) for a, b in vec] + [(zero, zero)]
        return [shifted[0]] + [c_add(s, v) for s, v in zip(shifted[1:], vec)]

    def axpy(coef, vec, base):
        base = list(base) + [(zero, zero)] * (len(vec) - len(base))
        moved = [c_add(b, c_mul(coef, v)) for v, b in zip(vec, base)]
        return moved + base[len(vec):]

    residual = [(one, zero)]
    direction = residual
    mapped = operate(direction)
    update = [(zero, zero)]
    for sweep in range(ITERS):
        weights = [
            c_sum([c_mul((m[0], -m[1]), gram(j, k)) for j, m in enumerate(mapped)])
            for k in range(min(len(mapped) + 1, ITERS + 1))
        ]
        norm = dot(weights[: len(mapped)], mapped)[0]
        mixed = dot(weights, residual)
        alpha = (mixed[0] / norm, mixed[1] / norm)
        update = axpy(alpha, direction, update)
        if sweep + 1 < ITERS:
            residual = axpy((-alpha[0], -alpha[1]), mapped, residual)
            fresh = operate(residual)
            turn = dot(weights, fresh)
            beta = (-turn[0] / norm, -turn[1] / norm)
            direction = axpy(beta, direction, residual)
            mapped = axpy(beta, mapped, fresh)
    return update


def kernel(
    n_space,
    n_src,
    background_hbm,
    warm_hbm,
    conductivity_hbm,
    frequencies,
    pair_freq,
    measured_hbm,
    layer_hbm,
    cell_hbm,
    component_hbm,
    adjoint,
    gradient,
    background,
    warm,
    conductivity,
    measured,
    layer,
    cell,
    component,
    hot,
    load_sem,
    basis,
    sums,
    above,
    below,
    source,
    measured_all,
    gram_rows,
    gram_all,
    shares,
    shares_in,
    halo_send,
    halo_recv,
    measured_send,
    measured_recv,
    gram_send,
    gram_recv,
    share_send,
    share_recv,
):
    me = lax.axis_index("space")
    pair = lax.axis_index("src")
    planes, rows_y, rows_z = conductivity.shape
    last = planes - 1

    barrier = pltpu.get_barrier_semaphore()
    for off in range(1, n_space):
        pl.semaphore_signal(
            barrier, 1, device_id={"space": lax.rem(me + off, n_space)}, device_id_type=MESH
        )
    for off in range(1, n_src):
        pl.semaphore_signal(
            barrier, 1, device_id={"src": lax.rem(pair + off, n_src)}, device_id_type=MESH
        )

    loads = [
        pltpu.make_async_copy(source_ref, target_ref, load_sem.at[index])
        for index, (source_ref, target_ref) in enumerate(
            [
                (warm_hbm, warm),
                (conductivity_hbm, conductivity),
                (layer_hbm, layer),
                (cell_hbm, cell),
                (component_hbm, component),
                (measured_hbm, measured),
                (background_hbm, background),
            ]
        )
    ]
    for load in loads:
        load.start()

    wave_k = frequencies[pair_freq[0]]

    @pl.when(me == 0)
    def _():
        below[...] = jnp.zeros_like(below)

    @pl.when(me == n_space - 1)
    def _():
        above[...] = jnp.zeros_like(above)

    loads[0].wait()
    for part in range(2):
        sum_y, sum_z = edge_sums(*[warm[part, 0, c][last:] for c in range(3)])
        sums[0, part, 0] = sum_y[0]
        sums[0, part, 1] = sum_z[0]

    pl.semaphore_wait(barrier, n_space - 1 + n_src - 1)

    def halo_copies(step):
        first = warm_hbm.at[:, 0, pl.ds(1, 2), 0] if step == 0 else basis.at[step - 1, :, pl.ds(1, 2), 0]
        upward = pltpu.make_async_remote_copy(
            src_ref=sums.at[step],
            dst_ref=below.at[step],
            send_sem=halo_send.at[step, 0],
            recv_sem=halo_recv.at[step, 0],
            device_id={"space": lax.rem(me + 1, n_space)},
            device_id_type=MESH,
        )
        downward = pltpu.make_async_remote_copy(
            src_ref=first,
            dst_ref=above.at[step],
            send_sem=halo_send.at[step, 1],
            recv_sem=halo_recv.at[step, 1],
            device_id={"space": lax.rem(me + n_space - 1, n_space)},
            device_id_type=MESH,
        )
        return upward, downward

    def start_halo(step):
        upward, downward = halo_copies(step)

        @pl.when(me < n_space - 1)
        def _():
            upward.start()

        @pl.when(me > 0)
        def _():
            downward.start()

    def wait_halo(step):
        upward, downward = halo_copies(step)

        @pl.when(me > 0)
        def _():
            upward.wait_recv()

        @pl.when(me < n_space - 1)
        def _():
            downward.wait_recv()

    def end_halo(step):
        upward, downward = halo_copies(step)

        @pl.when(me < n_space - 1)
        def _():
            upward.wait_send()

        @pl.when(me > 0)
        def _():
            downward.wait_send()

    def measured_copy(off):
        return pltpu.make_async_remote_copy(
            src_ref=measured_hbm,
            dst_ref=measured_all.at[off],
            send_sem=measured_send.at[off],
            recv_sem=measured_recv.at[off],
            device_id={"space": lax.rem(me + off, n_space)},
            device_id_type=MESH,
        )

    def gram_copy(off):
        return pltpu.make_async_remote_copy(
            src_ref=gram_all.at[me],
            dst_ref=gram_all.at[me],
            send_sem=gram_send.at[off],
            recv_sem=gram_recv.at[off],
            device_id={"space": lax.rem(me + off, n_space)},
            device_id_type=MESH,
        )

    def gram_arrival(off):
        return pltpu.make_async_remote_copy(
            src_ref=gram_all.at[me],
            dst_ref=gram_all.at[lax.rem(me + n_space - off, n_space)],
            send_sem=gram_send.at[off],
            recv_sem=gram_recv.at[off],
            device_id={"space": lax.rem(me + off, n_space)},
            device_id_type=MESH,
        )

    def share_copy(off):
        peer = lax.rem(pair + off, n_src)
        return pltpu.make_async_remote_copy(
            src_ref=shares.at[peer],
            dst_ref=shares_in.at[off],
            send_sem=share_send.at[off],
            recv_sem=share_recv.at[off],
            device_id={"src": peer},
            device_id_type=MESH,
        )

    for off in range(1, n_space):
        measured_copy(off).start()
    start_halo(0)

    for load in loads[1:6]:
        load.wait()
    damping = wave_k * conductivity[...]

    for part in range(2):
        curled = curl_curl(*[warm[part, 0, c] for c in range(3)])
        for c in range(3):
            turned = damping * warm[1 - part, 0, c]
            basis[0, part, c] = -(curled[c] - turned if part == 0 else curled[c] + turned)

    shift_z = rows_z.bit_length() - 1
    row_count = 3 * planes * rows_y
    sites = measured.shape[2]
    row_id = lax.broadcasted_iota(jnp.int32, (row_count, sites), 0)
    lane_id = lax.broadcasted_iota(jnp.int32, (rows_z, sites), 0)

    def sender(off):
        return pl.ds(lax.rem(me + n_space - off, n_space), 1)

    for off in range(n_space):
        row = component[sender(off), :] * (planes * rows_y) + lax.shift_right_logical(
            cell[sender(off), :], shift_z
        )
        row = jnp.where(layer[sender(off), :] == me, row, -1)
        hot[:, off * sites : (off + 1) * sites] = jnp.where(row_id == row, 1.0, 0.0).astype(
            jnp.bfloat16
        )
    for off in range(1, n_space):
        measured_copy(off).wait_recv()
    pieces = [[] for _ in range(6)]
    for off in range(n_space):
        lane_hit = lane_id == jnp.bitwise_and(cell[sender(off), :], rows_z - 1)
        for part in range(2):
            rest = measured[part] if off == 0 else measured_all[off, part]
            for piece in range(3):
                rounded = rest.astype(jnp.bfloat16).astype(jnp.float32)
                rest = rest - rounded
                pieces[part * 3 + piece].append(
                    jnp.where(lane_hit, rounded, 0.0).astype(jnp.bfloat16)
                )
    placed = lax.dot_general(
        hot[...],
        jnp.concatenate([jnp.concatenate(block, axis=1) for block in pieces], axis=0),
        (((1,), (1,)), ((), ())),
        preferred_element_type=jnp.float32,
    )
    for part in range(2):
        terms = [
            placed[:, index * rows_z : (index + 1) * rows_z]
            for index in range(part * 3, part * 3 + 3)
        ]
        total = (terms[0] + terms[1]) + terms[2]
        source[part] = total.reshape(3, planes, rows_y, rows_z)
    for part in range(2):
        for c in range(3):
            basis[0, part, c] = basis[0, part, c] + source[part, c]

    slots = gram_slots()
    cells = 3 * planes * rows_y

    def gram_column(k):
        for j in range(k + 1):
            left = [basis[j, part].reshape(cells, rows_z) for part in range(2)]
            right = [basis[k, part].reshape(cells, rows_z) for part in range(2)]
            spot = slots[j, k, 0]
            gram_rows[spot : spot + 1, :] = jnp.sum(
                left[0] * right[0] + left[1] * right[1], axis=0, keepdims=True
            )
            if j < k:
                spot = slots[j, k, 1]
                gram_rows[spot : spot + 1, :] = jnp.sum(
                    left[0] * right[1] - left[1] * right[0], axis=0, keepdims=True
                )

    def correct(step, sign):
        for part in range(2):
            over_y = sign * above[step, part, 0]
            over_z = sign * above[step, part, 1]
            slope = (over_y - down(over_y, 0, 0.0)) + (over_z - down(over_z, 1, 0.0))
            basis[step, part, 0, last] = basis[step, part, 0, last] + slope
            basis[step, part, 1, last] = basis[step, part, 1, last] - over_y
            basis[step, part, 2, last] = basis[step, part, 2, last] - over_z
            basis[step, part, 1, 0] = basis[step, part, 1, 0] - sign * below[step, part, 0]
            basis[step, part, 2, 0] = basis[step, part, 2, 0] - sign * below[step, part, 1]

    for k in range(ITERS + 1):
        wait_halo(k)
        correct(k, -1.0 if k == 0 else 1.0)
        if k < ITERS:
            for part in range(2):
                sum_y, sum_z = edge_sums(*[basis[k, part, c][last:] for c in range(3)])
                sums[k + 1, part, 0] = sum_y[0]
                sums[k + 1, part, 1] = sum_z[0]
            start_halo(k + 1)
            for part in range(2):
                curled = curl_curl(*[basis[k, part, c] for c in range(3)])
                for c in range(3):
                    turned = damping * basis[k, 1 - part, c]
                    moved = curled[c] - SHIFT * basis[k, part, c]
                    basis[k + 1, part, c] = moved - turned if part == 0 else moved + turned
        gram_column(k)

    count = len(slots)
    held = gram_rows.shape[0]
    lanes = lax.broadcasted_iota(jnp.int32, (held, rows_z), 1)
    rows = lax.broadcasted_iota(jnp.int32, (held, rows_z), 0)
    row_sums = jnp.sum(jnp.where(rows < count, gram_rows[...], 0.0), axis=1, keepdims=True)
    gram_all[me] = jnp.sum(jnp.where(lanes == rows, row_sums, 0.0), axis=0, keepdims=True)
    for off in range(1, n_space):
        gram_copy(off).start()
    for off in range(1, n_space):
        gram_arrival(off).wait_recv()
    total = gram_all[0]
    for index in range(1, n_space):
        total = total + gram_all[index]
    splat = {
        key: jnp.broadcast_to(total[:, spot : spot + 1], (8, rows_z)) for key, spot in slots.items()
    }

    def gram(j, k):
        real = splat[min(j, k), max(j, k), 0]
        if j == k:
            return real, jnp.zeros_like(real)
        imag = splat[min(j, k), max(j, k), 1]
        return real, imag if j < k else -imag

    update = combination(gram)
    loads[6].wait()

    local = None
    tiles = (planes * rows_y // 8, 8, rows_z)
    for c in range(3):
        real = warm[0, 0, c].reshape(tiles)
        imag = warm[1, 0, c].reshape(tiles)
        for k in range(ITERS):
            field_re = basis[k, 0, c].reshape(tiles)
            field_im = basis[k, 1, c].reshape(tiles)
            coef_re, coef_im = update[k][0][None], update[k][1][None]
            real = real + (coef_re * field_re - coef_im * field_im)
            imag = imag + (coef_re * field_im + coef_im * field_re)
        adjoint[0, 0, c] = real.reshape(planes, rows_y, rows_z)
        adjoint[1, 0, c] = imag.reshape(planes, rows_y, rows_z)
        term = real * background[1, 0, c].reshape(tiles) + imag * background[0, 0, c].reshape(tiles)
        local = term if local is None else local + term
    local = (wave_k * local).reshape(planes, rows_y, rows_z)
    share = rows_y // n_src
    for index in range(n_src):
        shares[index] = local[:, index * share : (index + 1) * share]
    for off in range(1, n_src):
        share_copy(off).start()
    for off in range(1, n_src):
        share_copy(off).wait_recv()
    result = shares[pair]
    for off in range(1, n_src):
        result = result + shares_in[off]
    gradient[...] = result

    for off in range(1, n_space):
        measured_copy(off).wait_send()
    for k in range(ITERS + 1):
        end_halo(k)
    for off in range(1, n_space):
        gram_copy(off).wait_send()
    for off in range(1, n_src):
        share_copy(off).wait_send()


def shards(
    n_space,
    n_src,
    background,
    warm_start,
    conductivity,
    frequencies,
    pair_freq,
    weighted_residual,
    datum_layer_index,
    receiver_flat_cell,
    receiver_component,
):
    planes, rows_y, rows_z = conductivity.shape
    sites = weighted_residual.shape[2]
    held = -(-len(gram_slots()) // 8) * 8
    vmem = pl.BlockSpec(memory_space=pltpu.VMEM)
    hbm = pl.BlockSpec(memory_space=pltpu.HBM)
    smem = pl.BlockSpec(memory_space=pltpu.SMEM)
    f32 = jnp.float32
    dma = pltpu.SemaphoreType.DMA
    return pl.pallas_call(
        functools.partial(kernel, n_space, n_src),
        out_shape=(
            pltpu.VMEM(warm_start.shape, f32),
            pltpu.VMEM((planes, rows_y // n_src, rows_z), f32),
        ),
        in_specs=[hbm, hbm, hbm, smem, smem, hbm, hbm, hbm, hbm],
        out_specs=(vmem, vmem),
        scratch_shapes=[
            pltpu.VMEM(background.shape, f32),
            pltpu.VMEM(warm_start.shape, f32),
            pltpu.VMEM(conductivity.shape, f32),
            pltpu.VMEM(weighted_residual.shape, f32),
            pltpu.VMEM((n_space, sites), jnp.int32),
            pltpu.VMEM((n_space, sites), jnp.int32),
            pltpu.VMEM((n_space, sites), jnp.int32),
            pltpu.VMEM((3 * planes * rows_y, n_space * sites), jnp.bfloat16),
            dma((7,)),
            pltpu.VMEM((ITERS + 1, 2, 3, planes, rows_y, rows_z), f32),
            pltpu.VMEM((ITERS + 1, 2, 2, rows_y, rows_z), f32),
            pltpu.VMEM((ITERS + 1, 2, 2, rows_y, rows_z), f32),
            pltpu.VMEM((ITERS + 1, 2, 2, rows_y, rows_z), f32),
            pltpu.VMEM((2, 3, planes, rows_y, rows_z), f32),
            pltpu.VMEM((n_space, 2, 1, sites), f32),
            pltpu.VMEM((held, rows_z), f32),
            pltpu.VMEM((n_space, 1, rows_z), f32),
            pltpu.VMEM((n_src, planes, rows_y // n_src, rows_z), f32),
            pltpu.VMEM((n_src, planes, rows_y // n_src, rows_z), f32),
            dma((ITERS + 1, 2)),
            dma((ITERS + 1, 2)),
            dma((n_space,)),
            dma((n_space,)),
            dma((n_space,)),
            dma((n_space,)),
            dma((n_src,)),
            dma((n_src,)),
        ],
        compiler_params=pltpu.CompilerParams(collective_id=0, has_side_effects=True),
    )(
        background,
        warm_start,
        conductivity,
        frequencies,
        pair_freq,
        weighted_residual,
        datum_layer_index.reshape(n_space, sites),
        receiver_flat_cell.reshape(n_space, sites),
        receiver_component.reshape(n_space, sites),
    )


def solution(mesh):
    placed = (
        P(None, "src", None, "space", None, None),
        P(None, "src", None, "space", None, None),
        P("space", None, None),
        P(),
        P("src"),
        P(None, "src", "space"),
        P(),
        P(),
        P(),
    )
    return jax.shard_map(
        functools.partial(shards, mesh.shape["space"], mesh.shape["src"]),
        mesh=mesh,
        in_specs=placed,
        out_specs=(P(None, "src", None, "space", None, None), P("space", "src", None)),
        check_vma=False,
    )
```

```python
import functools

import jax
import jax.numpy as jnp
from jax import lax
from jax.experimental import pallas as pl
from jax.experimental.pallas import tpu as pltpu
from jax.sharding import PartitionSpec as P

ITERS = 4
SHIFT = 6.0
MESH = pl.DeviceIdType.MESH


def up(field, axis):
    length = field.shape[axis]
    cell = lax.broadcasted_iota(jnp.int32, field.shape, axis)
    return jnp.where(cell == length - 1, 0.0, pltpu.roll(field, length - 1, axis))


def down(field, axis, first):
    cell = lax.broadcasted_iota(jnp.int32, field.shape, axis)
    return jnp.where(cell == 0, first, pltpu.roll(field, 1, axis))


def edge_sums(comp_x, comp_y, comp_z):
    return comp_y + (up(comp_x, 1) - comp_x), comp_z + (up(comp_x, 2) - comp_x)


def curl_curl(comp_x, comp_y, comp_z):
    zero = jnp.zeros_like(comp_x[:1])
    sum_y, sum_z = edge_sums(comp_x, comp_y, comp_z)
    mag_z = jnp.concatenate([comp_y[1:], zero]) - sum_y
    mag_y = sum_z - jnp.concatenate([comp_z[1:], zero])
    mag_x = (up(comp_z, 1) - comp_z) - (up(comp_y, 2) - comp_y)
    before_z = jnp.concatenate([comp_y[:1], mag_z[:-1]])
    before_y = jnp.concatenate([-comp_z[:1], mag_y[:-1]])
    out_x = (mag_z - down(mag_z, 1, -comp_x)) - (mag_y - down(mag_y, 2, comp_x))
    out_y = (mag_x - down(mag_x, 2, -comp_y)) - (mag_z - before_z)
    out_z = (mag_y - before_y) - (mag_x - down(mag_x, 1, comp_z))
    return out_x, out_y, out_z


def c_mul(a, b):
    return a[0] * b[0] - a[1] * b[1], a[0] * b[1] + a[1] * b[0]


def c_add(a, b):
    return a[0] + b[0], a[1] + b[1]


def c_sum(terms):
    total = terms[0]
    for term in terms[1:]:
        total = c_add(total, term)
    return total


def flipped(index, mask):
    result = index
    for bit in range(mask.bit_length()):
        if mask >> bit & 1:
            place = 1 << bit
            result = result + place - 2 * place * lax.rem(index // place, 2)
    return result


def gram_slots():
    slots = {}
    for k in range(ITERS + 1):
        for j in range(k + 1):
            slots[j, k, 0] = len(slots)
            if j < k:
                slots[j, k, 1] = len(slots)
    return slots


def combination(gram):
    zero = jnp.zeros_like(gram(0, 0)[0])
    one = zero + 1.0

    def dot(left, right):
        return c_sum([c_mul(a, b) for a, b in zip(left, right)])

    def operate(vec):
        shifted = [(SHIFT * a, SHIFT * b) for a, b in vec] + [(zero, zero)]
        return [shifted[0]] + [c_add(s, v) for s, v in zip(shifted[1:], vec)]

    def axpy(coef, vec, base):
        base = list(base) + [(zero, zero)] * (len(vec) - len(base))
        moved = [c_add(b, c_mul(coef, v)) for v, b in zip(vec, base)]
        return moved + base[len(vec):]

    residual = [(one, zero)]
    direction = residual
    mapped = operate(direction)
    update = [(zero, zero)]
    for sweep in range(ITERS):
        weights = [
            c_sum([c_mul((m[0], -m[1]), gram(j, k)) for j, m in enumerate(mapped)])
            for k in range(min(len(mapped) + 1, ITERS + 1))
        ]
        norm = dot(weights[: len(mapped)], mapped)[0]
        mixed = dot(weights, residual)
        alpha = (mixed[0] / norm, mixed[1] / norm)
        update = axpy(alpha, direction, update)
        if sweep + 1 < ITERS:
            residual = axpy((-alpha[0], -alpha[1]), mapped, residual)
            fresh = operate(residual)
            turn = dot(weights, fresh)
            beta = (-turn[0] / norm, -turn[1] / norm)
            direction = axpy(beta, direction, residual)
            mapped = axpy(beta, mapped, fresh)
    return update


def kernel(
    n_space,
    n_src,
    background_hbm,
    warm_hbm,
    conductivity_hbm,
    frequencies_hbm,
    pair_freq,
    measured_hbm,
    layer_hbm,
    cell_hbm,
    component_hbm,
    adjoint,
    gradient,
    background,
    warm,
    conductivity,
    frequencies,
    measured,
    layer,
    cell,
    component,
    hot,
    load_sem,
    basis,
    sums,
    above,
    below,
    source,
    measured_all,
    gram_rows,
    gram_all,
    shares,
    shares_in,
    halo_send,
    halo_recv,
    measured_send,
    measured_recv,
    gram_send,
    gram_recv,
    share_send,
    share_recv,
):
    me = lax.axis_index("space")
    pair = lax.axis_index("src")
    planes, rows_y, rows_z = conductivity.shape
    last = planes - 1

    barrier = pltpu.get_barrier_semaphore()
    for off in range(1, n_space):
        pl.semaphore_signal(
            barrier, 1, device_id={"space": lax.rem(me + off, n_space)}, device_id_type=MESH
        )
    for off in range(1, n_src):
        pl.semaphore_signal(
            barrier, 1, device_id={"src": lax.rem(pair + off, n_src)}, device_id_type=MESH
        )

    loads = [
        pltpu.make_async_copy(source_ref, target_ref, load_sem.at[index])
        for index, (source_ref, target_ref) in enumerate(
            [
                (warm_hbm, warm),
                (conductivity_hbm, conductivity),
                (layer_hbm, layer),
                (cell_hbm, cell),
                (component_hbm, component),
                (measured_hbm, measured),
                (background_hbm, background),
                (frequencies_hbm, frequencies),
            ]
        )
    ]
    for load in loads:
        load.start()

    @pl.when(me == 0)
    def _():
        below[...] = jnp.zeros_like(below)

    @pl.when(me == n_space - 1)
    def _():
        above[...] = jnp.zeros_like(above)

    loads[0].wait()
    for part in range(2):
        sum_y, sum_z = edge_sums(*[warm[part, 0, c][last:] for c in range(3)])
        sums[0, part, 0] = sum_y[0]
        sums[0, part, 1] = sum_z[0]

    pl.semaphore_wait(barrier, n_space - 1 + n_src - 1)

    def halo_copies(step):
        first = warm_hbm.at[:, 0, pl.ds(1, 2), 0] if step == 0 else basis.at[step - 1, :, pl.ds(1, 2), 0]
        upward = pltpu.make_async_remote_copy(
            src_ref=sums.at[step],
            dst_ref=below.at[step],
            send_sem=halo_send.at[step, 0],
            recv_sem=halo_recv.at[step, 0],
            device_id={"space": lax.rem(me + 1, n_space)},
            device_id_type=MESH,
        )
        downward = pltpu.make_async_remote_copy(
            src_ref=first,
            dst_ref=above.at[step],
            send_sem=halo_send.at[step, 1],
            recv_sem=halo_recv.at[step, 1],
            device_id={"space": lax.rem(me + n_space - 1, n_space)},
            device_id_type=MESH,
        )
        return upward, downward

    def start_halo(step):
        upward, downward = halo_copies(step)

        @pl.when(me < n_space - 1)
        def _():
            upward.start()

        @pl.when(me > 0)
        def _():
            downward.start()

    def wait_halo(step):
        upward, downward = halo_copies(step)

        @pl.when(me > 0)
        def _():
            upward.wait_recv()

        @pl.when(me < n_space - 1)
        def _():
            downward.wait_recv()

    def end_halo(step):
        upward, downward = halo_copies(step)

        @pl.when(me < n_space - 1)
        def _():
            upward.wait_send()

        @pl.when(me > 0)
        def _():
            downward.wait_send()

    def measured_copy(off):
        return pltpu.make_async_remote_copy(
            src_ref=measured_hbm,
            dst_ref=measured_all.at[off],
            send_sem=measured_send.at[off],
            recv_sem=measured_recv.at[off],
            device_id={"space": flipped(me, off)},
            device_id_type=MESH,
        )

    def gram_copy(mask):
        return pltpu.make_async_remote_copy(
            src_ref=gram_all.at[0],
            dst_ref=gram_all.at[mask],
            send_sem=gram_send.at[mask],
            recv_sem=gram_recv.at[mask],
            device_id={"space": flipped(me, mask)},
            device_id_type=MESH,
        )

    def share_copy(off):
        peer = lax.rem(pair + off, n_src)
        return pltpu.make_async_remote_copy(
            src_ref=shares.at[peer],
            dst_ref=shares_in.at[off],
            send_sem=share_send.at[off],
            recv_sem=share_recv.at[off],
            device_id={"src": peer},
            device_id_type=MESH,
        )

    for off in range(n_space - 1, 0, -1):
        measured_copy(off).start()
    start_halo(0)

    for load in loads[1:6] + loads[7:]:
        load.wait()
    wave_k = frequencies[pair_freq[0]]
    damping = wave_k * conductivity[...]

    for part in range(2):
        curled = curl_curl(*[warm[part, 0, c] for c in range(3)])
        for c in range(3):
            turned = damping * warm[1 - part, 0, c]
            basis[0, part, c] = -(curled[c] - turned if part == 0 else curled[c] + turned)

    shift_z = rows_z.bit_length() - 1
    row_count = 3 * planes * rows_y
    sites = measured.shape[2]
    row_id = lax.broadcasted_iota(jnp.int32, (row_count, sites), 0)
    lane_id = lax.broadcasted_iota(jnp.int32, (rows_z, sites), 0)

    def sender(off):
        return pl.ds(flipped(me, off), 1)

    for off in range(n_space):
        row = component[sender(off), :] * (planes * rows_y) + lax.shift_right_logical(
            cell[sender(off), :], shift_z
        )
        row = jnp.where(layer[sender(off), :] == me, row, -1)
        hot[:, off * sites : (off + 1) * sites] = jnp.where(row_id == row, 1.0, 0.0).astype(
            jnp.bfloat16
        )
    for off in range(1, n_space):
        measured_copy(off).wait_recv()
    pieces = [[] for _ in range(6)]
    for off in range(n_space):
        lane_hit = lane_id == jnp.bitwise_and(cell[sender(off), :], rows_z - 1)
        for part in range(2):
            rest = measured[part] if off == 0 else measured_all[off, part]
            for piece in range(3):
                rounded = rest.astype(jnp.bfloat16).astype(jnp.float32)
                rest = rest - rounded
                pieces[part * 3 + piece].append(
                    jnp.where(lane_hit, rounded, 0.0).astype(jnp.bfloat16)
                )
    placed = lax.dot_general(
        hot[...],
        jnp.concatenate([jnp.concatenate(block, axis=1) for block in pieces], axis=0),
        (((1,), (1,)), ((), ())),
        preferred_element_type=jnp.float32,
    )
    for part in range(2):
        terms = [
            placed[:, index * rows_z : (index + 1) * rows_z]
            for index in range(part * 3, part * 3 + 3)
        ]
        total = (terms[0] + terms[1]) + terms[2]
        source[part] = total.reshape(3, planes, rows_y, rows_z)
    for part in range(2):
        for c in range(3):
            basis[0, part, c] = basis[0, part, c] + source[part, c]

    slots = gram_slots()
    cells = 3 * planes * rows_y

    def gram_column(k):
        for j in range(k + 1):
            left = [basis[j, part].reshape(cells, rows_z) for part in range(2)]
            right = [basis[k, part].reshape(cells, rows_z) for part in range(2)]
            spot = slots[j, k, 0]
            gram_rows[spot : spot + 1, :] = jnp.sum(
                left[0] * right[0] + left[1] * right[1], axis=0, keepdims=True
            )
            if j < k:
                spot = slots[j, k, 1]
                gram_rows[spot : spot + 1, :] = jnp.sum(
                    left[0] * right[1] - left[1] * right[0], axis=0, keepdims=True
                )

    def correct(step, sign):
        for part in range(2):
            over_y = sign * above[step, part, 0]
            over_z = sign * above[step, part, 1]
            slope = (over_y - down(over_y, 0, 0.0)) + (over_z - down(over_z, 1, 0.0))
            basis[step, part, 0, last] = basis[step, part, 0, last] + slope
            basis[step, part, 1, last] = basis[step, part, 1, last] - over_y
            basis[step, part, 2, last] = basis[step, part, 2, last] - over_z
            basis[step, part, 1, 0] = basis[step, part, 1, 0] - sign * below[step, part, 0]
            basis[step, part, 2, 0] = basis[step, part, 2, 0] - sign * below[step, part, 1]

    for k in range(ITERS + 1):
        wait_halo(k)
        correct(k, -1.0 if k == 0 else 1.0)
        if k < ITERS:
            for part in range(2):
                sum_y, sum_z = edge_sums(*[basis[k, part, c][last:] for c in range(3)])
                sums[k + 1, part, 0] = sum_y[0]
                sums[k + 1, part, 1] = sum_z[0]
            start_halo(k + 1)
            for part in range(2):
                curled = curl_curl(*[basis[k, part, c] for c in range(3)])
                for c in range(3):
                    turned = damping * basis[k, 1 - part, c]
                    moved = curled[c] - SHIFT * basis[k, part, c]
                    basis[k + 1, part, c] = moved - turned if part == 0 else moved + turned
        gram_column(k)

    count = len(slots)
    held = gram_rows.shape[0]
    lanes = lax.broadcasted_iota(jnp.int32, (held, rows_z), 1)
    rows = lax.broadcasted_iota(jnp.int32, (held, rows_z), 0)
    row_sums = jnp.sum(jnp.where(rows < count, gram_rows[...], 0.0), axis=1, keepdims=True)
    gram_all[0] = jnp.sum(jnp.where(lanes == rows, row_sums, 0.0), axis=0, keepdims=True)
    gram_copies = [gram_copy(mask) for mask in range(n_space - 1, 0, -1)]
    for copy in gram_copies:
        copy.start()
    for copy in gram_copies:
        copy.wait_recv()
    level = [gram_all[mask] for mask in range(n_space)]
    while len(level) > 1:
        level = [level[i] + level[i + 1] for i in range(0, len(level), 2)]
    total = level[0]
    splat = {
        key: jnp.broadcast_to(total[:, spot : spot + 1], (8, rows_z)) for key, spot in slots.items()
    }

    def gram(j, k):
        real = splat[min(j, k), max(j, k), 0]
        if j == k:
            return real, jnp.zeros_like(real)
        imag = splat[min(j, k), max(j, k), 1]
        return real, imag if j < k else -imag

    update = combination(gram)
    loads[6].wait()

    local = None
    tiles = (planes * rows_y // 8, 8, rows_z)
    for c in range(3):
        real = warm[0, 0, c].reshape(tiles)
        imag = warm[1, 0, c].reshape(tiles)
        for k in range(ITERS):
            field_re = basis[k, 0, c].reshape(tiles)
            field_im = basis[k, 1, c].reshape(tiles)
            coef_re, coef_im = update[k][0][None], update[k][1][None]
            real = real + (coef_re * field_re - coef_im * field_im)
            imag = imag + (coef_re * field_im + coef_im * field_re)
        adjoint[0, 0, c] = real.reshape(planes, rows_y, rows_z)
        adjoint[1, 0, c] = imag.reshape(planes, rows_y, rows_z)
        term = real * background[1, 0, c].reshape(tiles) + imag * background[0, 0, c].reshape(tiles)
        local = term if local is None else local + term
    local = (wave_k * local).reshape(planes, rows_y, rows_z)
    share = rows_y // n_src
    for index in range(n_src):
        shares[index] = local[:, index * share : (index + 1) * share]
    for off in range(1, n_src):
        share_copy(off).start()
    for off in range(1, n_src):
        share_copy(off).wait_recv()
    result = shares[pair]
    for off in range(1, n_src):
        result = result + shares_in[off]
    gradient[...] = result

    for off in range(1, n_space):
        measured_copy(off).wait_send()
    for k in range(ITERS + 1):
        end_halo(k)
    for copy in gram_copies:
        copy.wait_send()
    for off in range(1, n_src):
        share_copy(off).wait_send()


def write_out(adjoint, gradient, adjoint_out, gradient_out, sems):
    copies = [
        pltpu.make_async_copy(adjoint, adjoint_out, sems.at[0]),
        pltpu.make_async_copy(gradient, gradient_out, sems.at[1]),
    ]
    for copy in copies:
        copy.start()
    for copy in copies:
        copy.wait()


def shards(
    n_space,
    n_src,
    background,
    warm_start,
    conductivity,
    frequencies,
    pair_freq,
    weighted_residual,
    datum_layer_index,
    receiver_flat_cell,
    receiver_component,
):
    planes, rows_y, rows_z = conductivity.shape
    sites = weighted_residual.shape[2]
    held = -(-len(gram_slots()) // 8) * 8
    vmem = pl.BlockSpec(memory_space=pltpu.VMEM)
    hbm = pl.BlockSpec(memory_space=pltpu.HBM)
    f32 = jnp.float32
    dma = pltpu.SemaphoreType.DMA
    results = pl.pallas_call(
        functools.partial(kernel, n_space, n_src),
        out_shape=(
            pltpu.VMEM(warm_start.shape, f32),
            pltpu.VMEM((planes, rows_y // n_src, rows_z), f32),
        ),
        in_specs=[hbm] * 4 + [pl.BlockSpec(memory_space=pltpu.SMEM)] + [hbm] * 4,
        out_specs=(vmem, vmem),
        scratch_shapes=[
            pltpu.VMEM(background.shape, f32),
            pltpu.VMEM(warm_start.shape, f32),
            pltpu.VMEM(conductivity.shape, f32),
            pltpu.SMEM(frequencies.shape, f32),
            pltpu.VMEM(weighted_residual.shape, f32),
            pltpu.VMEM((n_space, sites), jnp.int32),
            pltpu.VMEM((n_space, sites), jnp.int32),
            pltpu.VMEM((n_space, sites), jnp.int32),
            pltpu.VMEM((3 * planes * rows_y, n_space * sites), jnp.bfloat16),
            dma((8,)),
            pltpu.VMEM((ITERS + 1, 2, 3, planes, rows_y, rows_z), f32),
            pltpu.VMEM((ITERS + 1, 2, 2, rows_y, rows_z), f32),
            pltpu.VMEM((ITERS + 1, 2, 2, rows_y, rows_z), f32),
            pltpu.VMEM((ITERS + 1, 2, 2, rows_y, rows_z), f32),
            pltpu.VMEM((2, 3, planes, rows_y, rows_z), f32),
            pltpu.VMEM((n_space, 2, 1, sites), f32),
            pltpu.VMEM((held, rows_z), f32),
            pltpu.VMEM((n_space, 1, rows_z), f32),
            pltpu.VMEM((n_src, planes, rows_y // n_src, rows_z), f32),
            pltpu.VMEM((n_src, planes, rows_y // n_src, rows_z), f32),
            dma((ITERS + 1, 2)),
            dma((ITERS + 1, 2)),
            dma((n_space,)),
            dma((n_space,)),
            dma((n_space,)),
            dma((n_space,)),
            dma((n_src,)),
            dma((n_src,)),
        ],
        compiler_params=pltpu.CompilerParams(collective_id=0, has_side_effects=True),
    )(
        background,
        warm_start,
        conductivity,
        frequencies,
        pair_freq,
        weighted_residual,
        datum_layer_index.reshape(n_space, sites),
        receiver_flat_cell.reshape(n_space, sites),
        receiver_component.reshape(n_space, sites),
    )

    return pl.pallas_call(
        write_out,
        out_shape=(
            jax.ShapeDtypeStruct(warm_start.shape, f32),
            jax.ShapeDtypeStruct((planes, rows_y // n_src, rows_z), f32),
        ),
        in_specs=[vmem] * 2,
        out_specs=(hbm, hbm),
        scratch_shapes=[dma((2,))],
    )(*[pltpu.with_memory_space_constraint(result, pltpu.VMEM) for result in results])


def solution(mesh):
    placed = (
        P(None, "src", None, "space", None, None),
        P(None, "src", None, "space", None, None),
        P("space", None, None),
        P(),
        P("src"),
        P(None, "src", "space"),
        P(),
        P(),
        P(),
    )
    return jax.shard_map(
        functools.partial(shards, mesh.shape["space"], mesh.shape["src"]),
        mesh=mesh,
        in_specs=placed,
        out_specs=(P(None, "src", None, "space", None, None), P("space", "src", None)),
        check_vma=False,
    )
```
